32 devices in a mesh: dp: 2 (over y), space: 4 (over z), chan: 4 (over x, core).
Axes of the slice: x: 2, y: 2, z: 4, core: 2. Of those that a mesh axis runs over, the one named last changes fastest.
Arguments:
- volumes: bfloat16 [2, 8, 512, 1024], P('dp', 'space', 'chan'), may hold values from -6 to 6
- kernel: bfloat16 [512, 13824], P('chan'), may hold values from -0.15625 to 0.15625
- bias: float32 [512], P('chan'), may hold values from -3 to 3
- act_grad: bfloat16 [2, 4, 512, 256], P('dp', 'space', 'chan'), may hold values from -6 to 6
Outputs:
- activation: bfloat16 [2, 4, 512, 256], P('dp', 'space', 'chan')
- grad_x: bfloat16 [2, 8, 512, 1024], P('dp', 'space', 'chan')
- grad_w: float32 [512, 13824], P('chan')
- grad_b: float32 [512], P('chan')
The draws below stay inside these ranges and needn't reach their ends.
All inputs are finite; a program needn't handle non-finite values.
Results may differ from the reference program's by a relative error of at most 0.005.
Values may be sent and summed in bfloat16 or wider, within the bound.
A program may use at most 64 MiB of HBM per device.

```python
import jax
import jax.numpy as jnp
from jax import lax

CIN = 512
COUT = 512
GRID = 32
VOLUMES = 2
GX = 8
OX = 4
OG = 16
N_CHAN = 4


def shard_levels(key, shape, split, low, top_value):
    factor_of = 1.0
    for position, blocks in split:
        draws = jax.random.uniform(jax.random.fold_in(jax.random.fold_in(key, 6), position), (blocks,), jnp.float32, low / len(split), top_value / len(split))
        factor_of = factor_of * jnp.repeat(jnp.exp(draws), shape[position] // blocks).reshape((-1,) + (1,) * (len(shape) - 1 - position))
    return factor_of


def noise(own_key, extent, scale, most, split=(), held_as=jnp.bfloat16):
    array = scale * jax.random.normal(own_key, extent, jnp.float32)
    if split:
        array = array * shard_levels(own_key, extent, split, -0.22, 0.18)
    return jnp.clip(array, -most, most).astype(held_as)


def setup_inputs(seed: int = 0) -> dict:
    seeds = jax.random.split(jax.random.key(seed), 5)
    volumes = noise(seeds[0], (VOLUMES, GX, CIN, GRID * GRID), 1.0, 6.0, ((0, 2), (1, 4), (2, 4)))
    kernel = noise(seeds[1], (COUT, 27 * CIN), (27 * CIN // 8) ** -0.5, 0.15625, ((0, 4),))
    bias = noise(seeds[2], (COUT,), 0.5, 3.0, ((0, 4),), jnp.float32)
    act_grad = noise(seeds[3], (VOLUMES, OX, COUT, OG * OG), 1.0, 6.0, ((0, 2), (1, 4), (2, 4)))
    return dict(volumes=volumes, kernel=kernel, bias=bias, act_grad=act_grad)


NUMBERS = ('NDHWC', 'DHWIO', 'NDHWC')

def forward_conv(inputs, filters):
    return lax.conv_general_dilated(inputs, filters, (2, 2, 2), ((1, 1), (1, 1), (1, 1)), dimension_numbers=NUMBERS, preferred_element_type=jnp.float32)

def transpose_conv(grads, flipped):
    return lax.conv_general_dilated(grads, flipped, (1, 1, 1), ((1, 2), (1, 2), (1, 2)), lhs_dilation=(2, 2, 2), dimension_numbers=NUMBERS, preferred_element_type=jnp.float32)

def reference(volumes, kernel, bias, act_grad):
    total_vols = volumes.shape[0]
    vol_cells = volumes.reshape(total_vols, GX, CIN, GRID, GRID).transpose(0, 1, 3, 4, 2)
    filters = kernel.reshape(COUT, 3, 3, 3, CIN).transpose(1, 2, 3, 4, 0)
    grad_cells = act_grad.reshape(total_vols, OX, COUT, OG, OG).transpose(0, 1, 3, 4, 2)
    pre_act = forward_conv(vol_cells, filters) + bias
    activation = jax.nn.gelu(pre_act).astype(jnp.bfloat16)
    _, pull_back = jax.vjp(jax.nn.gelu, pre_act)
    out_grad = pull_back(grad_cells.astype(jnp.float32))[0].astype(jnp.bfloat16)
    group_width = COUT // N_CHAN
    flipped = filters[::-1, ::-1, ::-1].transpose(0, 1, 2, 4, 3)
    total = jnp.zeros(vol_cells.shape, jnp.float32)
    for group in range(N_CHAN):
        lower = group * group_width
        partial_grad = transpose_conv(out_grad[..., lower:lower + group_width], flipped[:, :, :, lower:lower + group_width, :])
        total = total + partial_grad
    grad_cells_x = total.astype(jnp.bfloat16)
    padded = jnp.pad(vol_cells, ((0, 0), (1, 1), (1, 1), (1, 1), (0, 0)))
    out_x, out_y, out_z = (out_grad.shape[1], out_grad.shape[2], out_grad.shape[3])
    flat_grad = out_grad.reshape(-1, COUT)
    tap_terms = []
    for first_tap in range(3):
        for second_tap in range(3):
            for third_tap in range(3):
                window = padded[:, first_tap:first_tap + 2 * out_x:2, second_tap:second_tap + 2 * out_y:2, third_tap:third_tap + 2 * out_z:2, :]
                tap_terms.append(lax.dot_general(window.reshape(-1, CIN), flat_grad, (((0,), (0,)), ((), ())), preferred_element_type=jnp.float32))
    weight_old = jnp.stack(tap_terms).reshape(3, 3, 3, CIN, COUT) / VOLUMES
    grad_b = lax.optimization_barrier(jnp.sum(out_grad.astype(jnp.float32), axis=(0, 1, 2, 3))) / VOLUMES
    activation_out = activation.transpose(0, 1, 4, 2, 3).reshape(total_vols, OX, COUT, OG * OG)
    grad_x = grad_cells_x.transpose(0, 1, 4, 2, 3).reshape(total_vols, GX, CIN, GRID * GRID)
    grad_w = weight_old.transpose(4, 0, 1, 2, 3).reshape(COUT, 27 * CIN)
    return (activation_out, grad_x, grad_w, grad_b)
```

```python
import functools

import jax
import jax.numpy as jnp
from jax import lax
from jax.experimental import pallas as pl
from jax.experimental.pallas import tpu as pltpu
from jax.sharding import PartitionSpec as P

GRID = 32
HALF = GRID // 2
CELLS = HALF * HALF
BF = jnp.bfloat16
F32 = jnp.float32
VM = pl.BlockSpec(memory_space=pltpu.VMEM)
TAPS = [(k1, k2, k3) for k1 in range(3) for k2 in range(3) for k3 in range(3)]


def phase_of(k2, k3):
    return 2 * (k2 != 1) + (k3 != 1)


def shift_of(k2, k3):
    return 2 * (k2 == 0) + (k3 == 0)


def parity_matrix():
    full = GRID * GRID
    dst = lax.broadcasted_iota(jnp.int32, (1, full), 1)
    phase, cell = dst // CELLS, dst % CELLS
    y = 2 * (cell // HALF) + phase // 2
    z = 2 * (cell % HALF) + phase % 2
    src = y * GRID + z
    rows = lax.broadcasted_iota(jnp.int32, (full, full), 0)
    return jnp.where(rows == src, 1.0, 0.0).astype(BF)


def lanes():
    return lax.broadcasted_iota(jnp.int32, (1, CELLS), 1)


def forward_shift(x, s):
    if s & 2:
        x = jnp.where(lanes() >= HALF, pltpu.roll(x, HALF, 1), 0.0)
    if s & 1:
        x = jnp.where(lanes() % HALF != 0, pltpu.roll(x, 1, 1), 0.0)
    return x


def backward_shift(x, s):
    if s & 2:
        x = jnp.where(lanes() < CELLS - HALF, pltpu.roll(x, CELLS - HALF, 1), 0.0)
    if s & 1:
        x = jnp.where(lanes() % HALF != HALF - 1, pltpu.roll(x, CELLS - 1, 1), 0.0)
    return x


def split_kernel(v_ref, p_ref, o_ref):
    o_ref[...] = jnp.dot(v_ref[...], p_ref[...], preferred_element_type=F32).astype(BF)


def merge_kernel(v_ref, p_ref, o_ref):
    o_ref[...] = lax.dot_general(
        v_ref[...], p_ref[...], (((1,), (1,)), ((), ())), preferred_element_type=F32
    ).astype(BF)


def forward_kernel(width, x_ref, w_ref, b_ref, g_ref, act_ref, dy_ref, db_ref):
    sums = [None] * 4
    for t, (k1, k2, k3) in enumerate(TAPS):
        ph, s = phase_of(k2, k3), shift_of(k2, k3)
        part = jnp.dot(
            w_ref[:, t * width : (t + 1) * width],
            x_ref[k1, :, ph * CELLS : (ph + 1) * CELLS],
            preferred_element_type=F32,
        )
        sums[s] = part if sums[s] is None else sums[s] + part
    u = b_ref[...] + sums[0]
    for s in (1, 2, 3):
        u = u + forward_shift(sums[s], s)
    c = 0.7978845608028654
    th = jnp.tanh(c * (u + 0.044715 * (u * u * u)))
    act_ref[...] = (0.5 * u * (1.0 + th)).astype(BF)
    slope = 0.5 * (1.0 + th) + 0.5 * u * (1.0 - th * th) * c * (1.0 + 3 * 0.044715 * u * u)
    dy = (g_ref[...].astype(F32) * slope).astype(BF)
    dy_ref[...] = dy
    db_ref[...] = jnp.sum(dy.astype(F32), axis=1, keepdims=True)


def shifted(dy):
    wide = dy.astype(F32)
    return [dy] + [backward_shift(wide, s).astype(BF) for s in (1, 2, 3)]


def weight_kernel(width, x_ref, dy_ref, dw_ref):
    views = shifted(dy_ref[...])
    for t, (k1, k2, k3) in enumerate(TAPS):
        ph, s = phase_of(k2, k3), shift_of(k2, k3)
        part = lax.dot_general(
            views[s],
            x_ref[k1, :, ph * CELLS : (ph + 1) * CELLS],
            (((1,), (1,)), ((), ())),
            preferred_element_type=F32,
        )
        dw_ref[:, t * width : (t + 1) * width] = part.astype(BF)


def input_kernel(width, w_ref, dy_ref, next_ref, gx_ref):
    own = shifted(dy_ref[...])
    following = shifted(next_ref[...])
    for plane in range(2):
        for ph in range(4):
            total = None
            for t, (k1, k2, k3) in enumerate(TAPS):
                if phase_of(k2, k3) != ph or (k1 == 1) != (plane == 0):
                    continue
                views = following if k1 == 0 else own
                part = lax.dot_general(
                    w_ref[:, t * width : (t + 1) * width],
                    views[shift_of(k2, k3)],
                    (((0,), (0,)), ((), ())),
                    preferred_element_type=F32,
                )
                total = part if total is None else total + part
            gx_ref[plane, :, ph * CELLS : (ph + 1) * CELLS] = total.astype(BF)


def call(kernel, out_shape, n_in, flops, moved):
    many = isinstance(out_shape, (tuple, list))
    return pl.pallas_call(
        kernel,
        out_shape=out_shape,
        in_specs=[VM] * n_in,
        out_specs=[VM] * len(out_shape) if many else VM,
        compiler_params=pltpu.CompilerParams(vmem_limit_bytes=48 << 20),
        cost_estimate=pl.CostEstimate(flops=flops, bytes_accessed=moved, transcendentals=0),
    )


def shape(*dims, dtype=BF):
    return jax.ShapeDtypeStruct(dims, dtype)


def from_behind(array, axis, by):
    size = lax.axis_size(axis)
    pairs = [(i, i + by) for i in range(size) if 0 <= i + by < size]
    return lax.ppermute(array, axis, pairs)


def per_device(volumes, kernel, bias, act_grad):
    batch, planes, part, cells = volumes.shape
    filters = kernel.shape[0]
    width = kernel.shape[1] // 27
    parity = parity_matrix()
    own = call(split_kernel, shape(planes * part, cells), 2, 2 * planes * part * cells**2, 1 << 20)(
        volumes.reshape(planes * part, cells), parity
    ).reshape(planes, part, cells)
    rim = from_behind(own[-1:], "space", 1)
    x_all = lax.all_gather(jnp.concatenate([rim, own], 0), "chan", axis=1, tiled=True)
    flops = 2 * 27 * width * filters * CELLS
    act, dy, db = call(
        functools.partial(forward_kernel, width),
        (shape(filters, CELLS), shape(filters, CELLS), shape(filters, 1, dtype=F32)),
        4,
        flops,
        7 << 20,
    )(x_all, kernel, bias.reshape(filters, 1), act_grad.reshape(filters, CELLS))
    dy_next = from_behind(dy, "space", -1)
    dw = call(functools.partial(weight_kernel, width), shape(filters, 27 * width), 2, flops, 7 << 20)(
        x_all, dy
    )
    gx = call(functools.partial(input_kernel, width), shape(planes, width, cells), 3, 2 * flops, 6 << 20)(
        kernel, dy, dy_next
    )
    count = batch * lax.axis_size("dp")
    dw_sum = lax.psum_scatter(dw, ("dp", "space"), scatter_dimension=0, tiled=True)
    dw_all = lax.all_gather(dw_sum, ("dp", "space"), axis=0, tiled=True)
    grad_w = dw_all.astype(F32) / count
    grad_b = lax.psum(db[:, 0], ("dp", "space")) / count
    gx_sum = lax.psum_scatter(gx, "chan", scatter_dimension=1, tiled=True)
    grad_x = call(merge_kernel, shape(planes * part, cells), 2, 2 * planes * part * cells**2, 1 << 20)(
        gx_sum.reshape(planes * part, cells), parity
    )
    return (
        act.reshape(act_grad.shape),
        grad_x.reshape(volumes.shape),
        grad_w,
        grad_b,
    )


def solution(mesh):
    in_specs = (
        P("dp", "space", "chan", None),
        P("chan", None),
        P("chan"),
        P("dp", "space", "chan", None),
    )
    out_specs = (
        P("dp", "space", "chan", None),
        P("dp", "space", "chan", None),
        P("chan", None),
        P("chan"),
    )
    return jax.shard_map(
        per_device, mesh=mesh, in_specs=in_specs, out_specs=out_specs, check_vma=False
    )
```

```python
import functools

import jax
import jax.numpy as jnp
from jax import lax
from jax.experimental import pallas as pl
from jax.experimental.pallas import tpu as pltpu
from jax.sharding import PartitionSpec as P

GRID = 32
HALF = GRID // 2
CELLS = HALF * HALF
BF = jnp.bfloat16
F32 = jnp.float32
VM = pl.BlockSpec(memory_space=pltpu.VMEM)
TAPS = [(k1, k2, k3) for k1 in range(3) for k2 in range(3) for k3 in range(3)]


def phase_of(k2, k3):
    return 2 * (k2 != 1) + (k3 != 1)


def shift_of(k2, k3):
    return 2 * (k2 == 0) + (k3 == 0)


def parity_matrix():
    full = GRID * GRID
    dst = lax.broadcasted_iota(jnp.int32, (1, full), 1)
    phase, cell = dst // CELLS, dst % CELLS
    y = 2 * (cell // HALF) + phase // 2
    z = 2 * (cell % HALF) + phase % 2
    src = y * GRID + z
    rows = lax.broadcasted_iota(jnp.int32, (full, full), 0)
    return jnp.where(rows == src, 1.0, 0.0).astype(BF)


def lanes():
    return lax.broadcasted_iota(jnp.int32, (1, CELLS), 1)


def forward_shift(x, s):
    if s & 2:
        x = jnp.where(lanes() >= HALF, pltpu.roll(x, HALF, 1), 0.0)
    if s & 1:
        x = jnp.where(lanes() % HALF != 0, pltpu.roll(x, 1, 1), 0.0)
    return x


def backward_shift(x, s):
    if s & 2:
        x = jnp.where(lanes() < CELLS - HALF, pltpu.roll(x, CELLS - HALF, 1), 0.0)
    if s & 1:
        x = jnp.where(lanes() % HALF != HALF - 1, pltpu.roll(x, CELLS - 1, 1), 0.0)
    return x


def split_kernel(v_ref, p_ref, o_ref):
    o_ref[...] = jnp.dot(v_ref[...], p_ref[...], preferred_element_type=F32).astype(BF)


def merge_kernel(v_ref, p_ref, o_ref):
    total = v_ref[0].astype(F32)
    for j in range(1, v_ref.shape[0]):
        total = total + v_ref[j].astype(F32)
    o_ref[...] = lax.dot_general(
        total.astype(BF).reshape(o_ref.shape), p_ref[...], (((1,), (1,)), ((), ())), preferred_element_type=F32
    ).astype(BF)


def send(src, dst, send_sem, recv_sem, device):
    return pltpu.make_async_remote_copy(
        src, dst, send_sem, recv_sem, device_id=device, device_id_type=pl.DeviceIdType.MESH
    )


def place():
    return lax.axis_index("dp"), lax.axis_index("space"), lax.axis_index("chan")


def greet(sizes):
    n_dp, n_space, n_chan = sizes
    y, z, c = place()
    barrier = pltpu.get_barrier_semaphore()
    g = y * n_space + z
    for o in range(1, n_chan):
        pl.semaphore_signal(
            barrier, 1, device_id=(y, z, (c + o) % n_chan), device_id_type=pl.DeviceIdType.MESH
        )
    for o in range(1, n_dp * n_space):
        h = (g + o) % (n_dp * n_space)
        pl.semaphore_signal(
            barrier, 1, device_id=(h // n_space, h % n_space, c), device_id_type=pl.DeviceIdType.MESH
        )
    pl.semaphore_wait(barrier, n_chan + n_dp * n_space - 2)


def gather_inputs(sizes, own_ref, x_ref, out_sem, in_sem, local_sem):
    n_dp, n_space, n_chan = sizes
    chips = n_chan // 2
    y, z, c = place()
    chip, core = c // 2, c % 2
    twin = (y, z, 2 * chip + 1 - core)
    greet(sizes)

    def planes(k):
        return pl.ds(1, 2) if k else pl.ds(0, 1)

    def block(k, j):
        return x_ref.at[planes(k), j]

    def to_chip(k, o, src):
        return send(
            src, block(k, c), out_sem.at[k, 0, o], in_sem.at[k, c],
            (y, z, 2 * ((chip + o) % chips) + core),
        )

    def to_twin(k, o, src):
        j = 2 * ((chip - o + chips) % chips) + core
        return send(src, block(k, j), out_sem.at[k, 1, o], in_sem.at[k, j], twin)

    def arrived(k, j):
        send(block(k, j), block(k, j), out_sem.at[k, 1, 0], in_sem.at[k, j], twin).wait_recv()

    rim = send(own_ref.at[pl.ds(1, 1)], block(0, c), out_sem.at[0, 2, 0], in_sem.at[0, c], (y, jnp.minimum(z + 1, n_space - 1), c))
    sends = [to_chip(1, o, own_ref) for o in range(1, chips)] + [to_twin(1, 0, own_ref)]

    @pl.when(z < n_space - 1)
    def _():
        rim.start()

    for copy in sends:
        copy.start()
    keep = pltpu.make_async_copy(own_ref, block(1, c), local_sem)
    keep.start()

    rim_out = [to_chip(0, o, block(0, c)) for o in range(1, chips)] + [to_twin(0, 0, block(0, c))]

    @pl.when(z > 0)
    def _():
        arrived(0, c)
        for copy in rim_out:
            copy.start()

    @pl.when(z == 0)
    def _():
        x_ref[0] = jnp.zeros_like(x_ref[0])

    for o in range(1, chips):
        j = 2 * ((chip - o + chips) % chips) + core
        arrived(1, j)
        passed = to_twin(1, o, block(1, j))
        passed.start()
        sends.append(passed)

    @pl.when(z > 0)
    def _():
        for o in range(1, chips):
            j = 2 * ((chip - o + chips) % chips) + core
            arrived(0, j)
            passed = to_twin(0, o, block(0, j))
            passed.start()
            rim_out.append(passed)
        for o in range(chips):
            arrived(0, 2 * ((chip - o + chips) % chips) + 1 - core)
        for copy in rim_out:
            copy.wait_send()

    for o in range(chips):
        arrived(1, 2 * ((chip - o + chips) % chips) + 1 - core)
    for copy in sends:
        copy.wait_send()

    @pl.when(z < n_space - 1)
    def _():
        rim.wait_send()

    keep.wait()


def forward_kernel(
    sizes, width, own_ref, w_ref, b_ref, g_ref, x_ref, act_ref, dy_ref, db_ref, out_sem, in_sem, local_sem
):
    gather_inputs(sizes, own_ref, x_ref, out_sem, in_sem, local_sem)
    sums = [None] * 4
    for t, (k1, k2, k3) in enumerate(TAPS):
        ph, s = phase_of(k2, k3), shift_of(k2, k3)
        part = jnp.dot(
            w_ref[:, t * width : (t + 1) * width],
            x_ref[k1, :, :, ph * CELLS : (ph + 1) * CELLS].reshape(width, CELLS),
            preferred_element_type=F32,
        )
        sums[s] = part if sums[s] is None else sums[s] + part
    u = b_ref[...] + sums[0]
    for s in (1, 2, 3):
        u = u + forward_shift(sums[s], s)
    c = 0.7978845608028654
    th = jnp.tanh(c * (u + 0.044715 * (u * u * u)))
    act_ref[...] = (0.5 * u * (1.0 + th)).astype(BF)
    slope = 0.5 * (1.0 + th) + 0.5 * u * (1.0 - th * th) * c * (1.0 + 3 * 0.044715 * u * u)
    dy = (g_ref[...].astype(F32) * slope).astype(BF)
    dy_ref[...] = dy
    db_ref[...] = lax.dot_general(
        jnp.ones((8, CELLS), BF), dy, (((1,), (1,)), ((), ())), preferred_element_type=F32
    )


def shifted(dy):
    wide = dy.astype(F32)
    return [dy] + [backward_shift(wide, s).astype(BF) for s in (1, 2, 3)]


def weight_kernel(width, x_ref, dy_ref, dw_ref):
    views = shifted(dy_ref[...])
    for t, (k1, k2, k3) in enumerate(TAPS):
        ph, s = phase_of(k2, k3), shift_of(k2, k3)
        part = lax.dot_general(
            views[s],
            x_ref[k1, :, :, ph * CELLS : (ph + 1) * CELLS].reshape(width, CELLS),
            (((1,), (1,)), ((), ())),
            preferred_element_type=F32,
        )
        dw_ref[:, t * width : (t + 1) * width] = part.astype(BF)


def input_kernel(width, w_ref, dy_ref, next_ref, gx_ref):
    own = shifted(dy_ref[...])
    following = shifted(next_ref[...])
    for plane in range(2):
        for ph in range(4):
            total = None
            for t, (k1, k2, k3) in enumerate(TAPS):
                if phase_of(k2, k3) != ph or (k1 == 1) != (plane == 0):
                    continue
                views = following if k1 == 0 else own
                part = lax.dot_general(
                    w_ref[:, t * width : (t + 1) * width],
                    views[shift_of(k2, k3)],
                    (((0,), (0,)), ((), ())),
                    preferred_element_type=F32,
                )
                total = part if total is None else total + part
            gx_ref[:, plane, :, ph * CELLS : (ph + 1) * CELLS] = total.astype(BF).reshape(
                gx_ref.shape[0], gx_ref.shape[2], CELLS
            )


def share_kernel(
    sizes, dw_ref, gx_ref, db_ref, all_ref, parts_ref, dbs_ref, out_sem, in_sem, gx_out, gx_in, db_out, db_in, local_sem
):
    n_dp, n_space, n_chan = sizes
    group = n_dp * n_space
    y, z, c = place()
    g = y * n_space + z
    greet(sizes)
    right = (y, jnp.minimum(z + 1, n_space - 1), c)
    left = (y, jnp.maximum(z - 1, 0), c)
    across = (1 - y, z, c)

    def hop(way, device, j, src=None):
        slot = all_ref.at[y * n_space + j]
        return send(slot if src is None else src, slot, out_sem.at[way, j], in_sem.at[y * n_space + j], device)

    def arrived(h):
        send(all_ref.at[h], all_ref.at[h], out_sem.at[2, 0], in_sem.at[h], across).wait_recv()

    locals_ = [
        pltpu.make_async_copy(dw_ref, all_ref.at[g], local_sem.at[0]),
        pltpu.make_async_copy(gx_ref.at[c], parts_ref.at[c], local_sem.at[1]),
        pltpu.make_async_copy(db_ref, dbs_ref.at[g], local_sem.at[2]),
    ]

    @pl.when(z < n_space - 1)
    def _():
        hop(0, right, z, dw_ref).start()

    @pl.when(z > 0)
    def _():
        hop(1, left, z, dw_ref).start()

    hop(2, across, z, dw_ref).start()
    extra = []
    for o in range(1, n_chan):
        to = (c + o) % n_chan
        extra.append(
            send(gx_ref.at[to], parts_ref.at[c], gx_out.at[o], gx_in.at[o], (y, z, to))
        )
    for o in range(1, group):
        to = (g + o) % group
        extra.append(
            send(db_ref, dbs_ref.at[g], db_out.at[o], db_in.at[o], (to // n_space, to % n_space, c))
        )
    for copy in extra:
        copy.start()
    for copy in locals_:
        copy.start()

    for d in range(1, n_space):
        @pl.when(z - d >= 0)
        def _():
            j = jnp.maximum(z - d, 0)
            arrived(y * n_space + j)

            @pl.when(z < n_space - 1)
            def _():
                hop(0, right, j).start()

            hop(2, across, j).start()

        @pl.when(z + d < n_space)
        def _():
            j = jnp.minimum(z + d, n_space - 1)
            arrived(y * n_space + j)

            @pl.when(z > 0)
            def _():
                hop(1, left, j).start()

            hop(2, across, j).start()

    for o in range(1, n_chan):
        frm = (c - o + n_chan) % n_chan
        send(parts_ref.at[frm], parts_ref.at[frm], gx_out.at[o], gx_in.at[o], (y, z, frm)).wait_recv()
    for o in range(1, group):
        frm = (g - o + group) % group
        send(dbs_ref.at[frm], dbs_ref.at[frm], db_out.at[o], db_in.at[o], (frm // n_space, frm % n_space, c)).wait_recv()
    for j in range(n_space):
        arrived((1 - y) * n_space + j)
        hop(2, across, j).wait_send()

        @pl.when((j <= z) & (z < n_space - 1))
        def _():
            hop(0, right, j).wait_send()

        @pl.when((j >= z) & (z > 0))
        def _():
            hop(1, left, j).wait_send()

    for copy in extra:
        copy.wait_send()
    for copy in locals_:
        copy.wait()


def call(kernel, out_shape, n_in, flops, moved, scratch=(), collective_id=None):
    many = isinstance(out_shape, (tuple, list))
    return pl.pallas_call(
        kernel,
        out_shape=out_shape,
        in_specs=[VM] * n_in,
        out_specs=[VM] * len(out_shape) if many else VM,
        scratch_shapes=scratch,
        compiler_params=pltpu.CompilerParams(
            vmem_limit_bytes=48 << 20,
            collective_id=collective_id,
            has_side_effects=collective_id is not None,
        ),
        cost_estimate=pl.CostEstimate(flops=flops, bytes_accessed=moved, transcendentals=0),
    )


def shape(*dims, dtype=BF):
    return jax.ShapeDtypeStruct(dims, dtype)


def from_behind(array, axis, by):
    size = lax.axis_size(axis)
    pairs = [(i, i + by) for i in range(size) if 0 <= i + by < size]
    return lax.ppermute(array, axis, pairs)


def per_device(volumes, kernel, bias, act_grad):
    batch, planes, part, cells = volumes.shape
    filters = kernel.shape[0]
    width = kernel.shape[1] // 27
    parity = parity_matrix()
    own = call(split_kernel, shape(planes * part, cells), 2, 2 * planes * part * cells**2, 1 << 20)(
        volumes.reshape(planes * part, cells), parity
    ).reshape(planes, part, cells)
    sizes = tuple(lax.axis_size(a) for a in ("dp", "space", "chan"))
    group, n_chan = sizes[0] * sizes[1], sizes[2]
    dma = pltpu.SemaphoreType.DMA
    flops = 2 * 27 * width * filters * CELLS
    x_all, act, dy, db = call(
        functools.partial(forward_kernel, sizes, width),
        (
            shape(3, n_chan, part, cells),
            shape(filters, CELLS),
            shape(filters, CELLS),
            shape(8, filters, dtype=F32),
        ),
        4,
        flops,
        10 << 20,
        scratch=(dma((2, 3, n_chan // 2)), dma((2, n_chan)), dma),
        collective_id=0,
    )(own, kernel, bias.reshape(filters, 1), act_grad.reshape(filters, CELLS))
    dy_next = from_behind(dy, "space", -1)
    dw = call(functools.partial(weight_kernel, width), shape(filters, 27 * width), 2, flops, 7 << 20)(
        x_all, dy
    )
    gx = call(functools.partial(input_kernel, width), shape(n_chan, planes, part, cells), 3, 2 * flops, 6 << 20)(
        kernel, dy, dy_next
    )
    count = batch * lax.axis_size("dp")
    dw_sum = lax.psum_scatter(dw, ("dp", "space"), scatter_dimension=0, tiled=True)
    dw_all, parts, dbs = call(
        functools.partial(share_kernel, sizes),
        (
            shape(group, *dw_sum.shape),
            shape(n_chan, planes, part, cells),
            shape(group, 8, filters, dtype=F32),
        ),
        3,
        0,
        12 << 20,
        scratch=(
            dma((3, sizes[1])),
            dma((group,)),
            dma((n_chan,)),
            dma((n_chan,)),
            dma((group,)),
            dma((group,)),
            dma((3,)),
        ),
        collective_id=1,
    )(dw_sum, gx, db)
    grad_w = dw_all.reshape(filters, 27 * width).astype(F32) / count
    grad_b = jnp.sum(dbs[:, 0], axis=0) / count
    grad_x = call(merge_kernel, shape(planes * part, cells), 2, 2 * planes * part * cells**2, 1 << 20)(
        parts, parity
    )
    return (
        act.reshape(act_grad.shape),
        grad_x.reshape(volumes.shape),
        grad_w,
        grad_b,
    )


def solution(mesh):
    in_specs = (
        P("dp", "space", "chan", None),
        P("chan", None),
        P("chan"),
        P("dp", "space", "chan", None),
    )
    out_specs = (
        P("dp", "space", "chan", None),
        P("dp", "space", "chan", None),
        P("chan", None),
        P("chan"),
    )
    return jax.shard_map(
        per_device, mesh=mesh, in_specs=in_specs, out_specs=out_specs, check_vma=False
    )
```

```python
import functools

import jax
import jax.numpy as jnp
from jax import lax
from jax.experimental import pallas as pl
from jax.experimental.pallas import tpu as pltpu
from jax.sharding import PartitionSpec as P

GRID = 32
HALF = GRID // 2
CELLS = HALF * HALF
BF = jnp.bfloat16
F32 = jnp.float32
VM = pl.BlockSpec(memory_space=pltpu.VMEM)
TAPS = [(k1, k2, k3) for k1 in range(3) for k2 in range(3) for k3 in range(3)]


def phase_of(k2, k3):
    return 2 * (k2 != 1) + (k3 != 1)


def shift_of(k2, k3):
    return 2 * (k2 == 0) + (k3 == 0)


def parity_matrix():
    full = GRID * GRID
    dst = lax.broadcasted_iota(jnp.int32, (1, full), 1)
    phase, cell = dst // CELLS, dst % CELLS
    y = 2 * (cell // HALF) + phase // 2
    z = 2 * (cell % HALF) + phase % 2
    src = y * GRID + z
    rows = lax.broadcasted_iota(jnp.int32, (full, full), 0)
    return jnp.where(rows == src, 1.0, 0.0).astype(BF)


def lanes():
    return lax.broadcasted_iota(jnp.int32, (1, CELLS), 1)


def forward_shift(x, s):
    if s & 2:
        x = jnp.where(lanes() >= HALF, pltpu.roll(x, HALF, 1), 0.0)
    if s & 1:
        x = jnp.where(lanes() % HALF != 0, pltpu.roll(x, 1, 1), 0.0)
    return x


def backward_shift(x, s):
    if s & 2:
        x = jnp.where(lanes() < CELLS - HALF, pltpu.roll(x, CELLS - HALF, 1), 0.0)
    if s & 1:
        x = jnp.where(lanes() % HALF != HALF - 1, pltpu.roll(x, CELLS - 1, 1), 0.0)
    return x


def split_kernel(v_ref, p_ref, o_ref):
    o_ref[...] = jnp.dot(v_ref[...], p_ref[...], preferred_element_type=F32).astype(BF)


def merge_kernel(v_ref, p_ref, o_ref):
    total = v_ref[0].astype(F32)
    for j in range(1, v_ref.shape[0]):
        total = total + v_ref[j].astype(F32)
    o_ref[...] = lax.dot_general(
        total.astype(BF).reshape(o_ref.shape), p_ref[...], (((1,), (1,)), ((), ())), preferred_element_type=F32
    ).astype(BF)


def send(src, dst, send_sem, recv_sem, device):
    return pltpu.make_async_remote_copy(
        src, dst, send_sem, recv_sem, device_id=device, device_id_type=pl.DeviceIdType.MESH
    )


def place():
    return lax.axis_index("dp"), lax.axis_index("space"), lax.axis_index("chan")


def greet(sizes):
    n_dp, n_space, n_chan = sizes
    y, z, c = place()
    barrier = pltpu.get_barrier_semaphore()
    g = y * n_space + z
    for o in range(1, n_chan):
        pl.semaphore_signal(
            barrier, 1, device_id=(y, z, (c + o) % n_chan), device_id_type=pl.DeviceIdType.MESH
        )
    for o in range(1, n_dp * n_space):
        h = (g + o) % (n_dp * n_space)
        pl.semaphore_signal(
            barrier, 1, device_id=(h // n_space, h % n_space, c), device_id_type=pl.DeviceIdType.MESH
        )
    pl.semaphore_wait(barrier, n_chan + n_dp * n_space - 2)


def gather_inputs(sizes, own_ref, x_ref, out_sem, in_sem, local_sem):
    n_dp, n_space, n_chan = sizes
    chips = n_chan // 2
    y, z, c = place()
    chip, core = c // 2, c % 2
    twin = (y, z, 2 * chip + 1 - core)
    greet(sizes)

    def planes(k):
        return pl.ds(1, 2) if k else pl.ds(0, 1)

    def block(k, j):
        return x_ref.at[planes(k), j]

    def to_chip(k, o, src):
        return send(
            src, block(k, c), out_sem.at[k, 0, o], in_sem.at[k, c],
            (y, z, 2 * ((chip + o) % chips) + core),
        )

    def to_twin(k, o, src):
        j = 2 * ((chip - o + chips) % chips) + core
        return send(src, block(k, j), out_sem.at[k, 1, o], in_sem.at[k, j], twin)

    def arrived(k, j):
        send(block(k, j), block(k, j), out_sem.at[k, 1, 0], in_sem.at[k, j], twin).wait_recv()

    rim = send(own_ref.at[pl.ds(1, 1)], block(0, c), out_sem.at[0, 2, 0], in_sem.at[0, c], (y, jnp.minimum(z + 1, n_space - 1), c))
    sends = [to_chip(1, o, own_ref) for o in range(1, chips)] + [to_twin(1, 0, own_ref)]

    @pl.when(z < n_space - 1)
    def _():
        rim.start()

    for copy in sends:
        copy.start()
    keep = pltpu.make_async_copy(own_ref, block(1, c), local_sem)
    keep.start()

    rim_out = [to_chip(0, o, block(0, c)) for o in range(1, chips)] + [to_twin(0, 0, block(0, c))]

    @pl.when(z > 0)
    def _():
        arrived(0, c)
        for copy in rim_out:
            copy.start()

    @pl.when(z == 0)
    def _():
        x_ref[0] = jnp.zeros_like(x_ref[0])

    for o in range(1, chips):
        j = 2 * ((chip - o + chips) % chips) + core
        arrived(1, j)
        passed = to_twin(1, o, block(1, j))
        passed.start()
        sends.append(passed)

    @pl.when(z > 0)
    def _():
        for o in range(1, chips):
            j = 2 * ((chip - o + chips) % chips) + core
            arrived(0, j)
            passed = to_twin(0, o, block(0, j))
            passed.start()
            rim_out.append(passed)
        for o in range(chips):
            arrived(0, 2 * ((chip - o + chips) % chips) + 1 - core)
        for copy in rim_out:
            copy.wait_send()

    for o in range(chips):
        arrived(1, 2 * ((chip - o + chips) % chips) + 1 - core)
    for copy in sends:
        copy.wait_send()

    @pl.when(z < n_space - 1)
    def _():
        rim.wait_send()

    keep.wait()


def forward_kernel(
    sizes, width, own_ref, w_ref, b_ref, g_ref, x_ref, act_ref, dy_ref, db_ref, out_sem, in_sem, local_sem
):
    gather_inputs(sizes, own_ref, x_ref, out_sem, in_sem, local_sem)
    sums = [None] * 4
    for t, (k1, k2, k3) in enumerate(TAPS):
        ph, s = phase_of(k2, k3), shift_of(k2, k3)
        part = jnp.dot(
            w_ref[:, t * width : (t + 1) * width],
            x_ref[k1, :, :, ph * CELLS : (ph + 1) * CELLS].reshape(width, CELLS),
            preferred_element_type=F32,
        )
        sums[s] = part if sums[s] is None else sums[s] + part
    u = b_ref[...] + sums[0]
    for s in (1, 2, 3):
        u = u + forward_shift(sums[s], s)
    c = 0.7978845608028654
    th = jnp.tanh(c * (u + 0.044715 * (u * u * u)))
    act_ref[...] = (0.5 * u * (1.0 + th)).astype(BF)
    slope = 0.5 * (1.0 + th) + 0.5 * u * (1.0 - th * th) * c * (1.0 + 3 * 0.044715 * u * u)
    dy = (g_ref[...].astype(F32) * slope).astype(BF)
    dy_ref[...] = dy
    db_ref[...] = lax.dot_general(
        jnp.ones((8, CELLS), BF), dy, (((1,), (1,)), ((), ())), preferred_element_type=F32
    )


def shifted(dy):
    wide = dy.astype(F32)
    return [dy] + [backward_shift(wide, s).astype(BF) for s in (1, 2, 3)]


def grads_kernel(sizes, width, x_ref, w_ref, dy_ref, dw_ref, gx_ref, next_ref, out_sem, in_sem):
    n_space = sizes[1]
    y, z, c = place()
    greet(sizes)
    back = send(dy_ref, next_ref, out_sem, in_sem, (y, jnp.maximum(z - 1, 0), c))

    @pl.when(z > 0)
    def _():
        back.start()

    own = shifted(dy_ref[...])
    for t, (k1, k2, k3) in enumerate(TAPS):
        ph, s = phase_of(k2, k3), shift_of(k2, k3)
        part = lax.dot_general(
            own[s],
            x_ref[k1, :, :, ph * CELLS : (ph + 1) * CELLS].reshape(width, CELLS),
            (((1,), (1,)), ((), ())),
            preferred_element_type=F32,
        )
        dw_ref[:, t * width : (t + 1) * width] = part.astype(BF)

    @pl.when(z < n_space - 1)
    def _():
        back.wait_recv()

    @pl.when(z == n_space - 1)
    def _():
        next_ref[...] = jnp.zeros_like(next_ref)

    following = shifted(next_ref[...])
    for plane in range(2):
        for ph in range(4):
            total = None
            for t, (k1, k2, k3) in enumerate(TAPS):
                if phase_of(k2, k3) != ph or (k1 == 1) != (plane == 0):
                    continue
                views = following if k1 == 0 else own
                part = lax.dot_general(
                    w_ref[:, t * width : (t + 1) * width],
                    views[shift_of(k2, k3)],
                    (((0,), (0,)), ((), ())),
                    preferred_element_type=F32,
                )
                total = part if total is None else total + part
            gx_ref[:, plane, :, ph * CELLS : (ph + 1) * CELLS] = total.astype(BF).reshape(
                gx_ref.shape[0], gx_ref.shape[2], CELLS
            )

    @pl.when(z > 0)
    def _():
        back.wait_send()


def share_kernel(
    sizes, dw_ref, gx_ref, db_ref, all_ref, parts_ref, dbs_ref, y_ref, r_ref, l_ref, s_ref,
    out_sem, in_sem, gx_out, gx_in, db_out, db_in, local_sem, y_out, y_in, z_out, r_in, l_in
):
    n_dp, n_space, n_chan = sizes
    group = n_dp * n_space
    y, z, c = place()
    g = y * n_space + z
    greet(sizes)
    right = (y, jnp.minimum(z + 1, n_space - 1), c)
    left = (y, jnp.maximum(z - 1, 0), c)
    across = (1 - y, z, c)

    def hop(way, device, j, src=None):
        slot = all_ref.at[y * n_space + j]
        return send(slot if src is None else src, slot, out_sem.at[way, j], in_sem.at[y * n_space + j], device)

    def arrived(h):
        send(all_ref.at[h], all_ref.at[h], out_sem.at[2, 0], in_sem.at[h], across).wait_recv()

    locals_ = [
        pltpu.make_async_copy(gx_ref.at[c], parts_ref.at[c], local_sem.at[1]),
        pltpu.make_async_copy(db_ref, dbs_ref.at[g], local_sem.at[2]),
    ]

    def over(j):
        return send(dw_ref.at[(1 - y) * n_space + j], y_ref.at[j], y_out.at[j], y_in.at[j], across)

    def rightward(j):
        return send(s_ref.at[j], r_ref.at[j], z_out.at[j], r_in.at[j], right)

    def leftward(j):
        return send(s_ref.at[j], l_ref.at[j], z_out.at[j], l_in.at[j], left)

    def both(j):
        over(j).wait_recv()
        return dw_ref[y * n_space + j].astype(F32) + y_ref[j].astype(F32)

    for d in range(n_space - 1, 0, -1):
        @pl.when(z + d < n_space)
        def _():
            over(jnp.minimum(z + d, n_space - 1)).start()

        @pl.when(z - d >= 0)
        def _():
            over(jnp.maximum(z - d, 0)).start()

    over(z).start()
    extra = []
    for o in range(1, n_chan):
        to = (c + o) % n_chan
        extra.append(
            send(gx_ref.at[to], parts_ref.at[c], gx_out.at[o], gx_in.at[o], (y, z, to))
        )
    for o in range(1, group):
        to = (g + o) % group
        extra.append(
            send(db_ref, dbs_ref.at[g], db_out.at[o], db_in.at[o], (to // n_space, to % n_space, c))
        )
    for copy in extra:
        copy.start()
    for copy in locals_:
        copy.start()

    for d in range(n_space - 1, 0, -1):
        @pl.when(z + d < n_space)
        def _():
            j = jnp.minimum(z + d, n_space - 1)
            mine = both(j)

            @pl.when(z == 0)
            def _():
                s_ref[j] = mine.astype(BF)

            @pl.when(z > 0)
            def _():
                rightward(j).wait_recv()
                s_ref[j] = (mine + r_ref[j].astype(F32)).astype(BF)

            rightward(j).start()

        @pl.when(z - d >= 0)
        def _():
            j = jnp.maximum(z - d, 0)
            mine = both(j)

            @pl.when(z == n_space - 1)
            def _():
                s_ref[j] = mine.astype(BF)

            @pl.when(z < n_space - 1)
            def _():
                leftward(j).wait_recv()
                s_ref[j] = (mine + l_ref[j].astype(F32)).astype(BF)

            leftward(j).start()

    @pl.when(z == 0)
    def _():
        r_ref[z] = jnp.zeros_like(r_ref[z])

    @pl.when(z == n_space - 1)
    def _():
        l_ref[z] = jnp.zeros_like(l_ref[z])

    @pl.when(z > 0)
    def _():
        rightward(z).wait_recv()

    @pl.when(z < n_space - 1)
    def _():
        leftward(z).wait_recv()

    all_ref[g] = (both(z) + r_ref[z].astype(F32) + l_ref[z].astype(F32)).astype(BF)

    @pl.when(z < n_space - 1)
    def _():
        hop(0, right, z).start()

    @pl.when(z > 0)
    def _():
        hop(1, left, z).start()

    hop(2, across, z).start()

    for d in range(1, n_space):
        @pl.when(z - d >= 0)
        def _():
            j = jnp.maximum(z - d, 0)
            arrived(y * n_space + j)

            @pl.when(z < n_space - 1)
            def _():
                hop(0, right, j).start()

            hop(2, across, j).start()

        @pl.when(z + d < n_space)
        def _():
            j = jnp.minimum(z + d, n_space - 1)
            arrived(y * n_space + j)

            @pl.when(z > 0)
            def _():
                hop(1, left, j).start()

            hop(2, across, j).start()

    for o in range(1, n_chan):
        frm = (c - o + n_chan) % n_chan
        send(parts_ref.at[frm], parts_ref.at[frm], gx_out.at[o], gx_in.at[o], (y, z, frm)).wait_recv()
    for o in range(1, group):
        frm = (g - o + group) % group
        send(dbs_ref.at[frm], dbs_ref.at[frm], db_out.at[o], db_in.at[o], (frm // n_space, frm % n_space, c)).wait_recv()
    for j in range(n_space):
        arrived((1 - y) * n_space + j)
        hop(2, across, j).wait_send()

        @pl.when((j <= z) & (z < n_space - 1))
        def _():
            hop(0, right, j).wait_send()

        @pl.when((j >= z) & (z > 0))
        def _():
            hop(1, left, j).wait_send()

        over(j).wait_send()

        @pl.when(j > z)
        def _():
            rightward(j).wait_send()

        @pl.when(j < z)
        def _():
            leftward(j).wait_send()

    for copy in extra:
        copy.wait_send()
    for copy in locals_:
        copy.wait()


def call(kernel, out_shape, n_in, flops, moved, scratch=(), collective_id=None):
    many = isinstance(out_shape, (tuple, list))
    return pl.pallas_call(
        kernel,
        out_shape=out_shape,
        in_specs=[VM] * n_in,
        out_specs=[VM] * len(out_shape) if many else VM,
        scratch_shapes=scratch,
        compiler_params=pltpu.CompilerParams(
            vmem_limit_bytes=48 << 20,
            collective_id=collective_id,
            has_side_effects=collective_id is not None,
        ),
        cost_estimate=pl.CostEstimate(flops=flops, bytes_accessed=moved, transcendentals=0),
    )


def shape(*dims, dtype=BF):
    return jax.ShapeDtypeStruct(dims, dtype)


def per_device(volumes, kernel, bias, act_grad):
    batch, planes, part, cells = volumes.shape
    filters = kernel.shape[0]
    width = kernel.shape[1] // 27
    parity = parity_matrix()
    own = call(split_kernel, shape(planes * part, cells), 2, 2 * planes * part * cells**2, 1 << 20)(
        volumes.reshape(planes * part, cells), parity
    ).reshape(planes, part, cells)
    sizes = tuple(lax.axis_size(a) for a in ("dp", "space", "chan"))
    group, n_chan = sizes[0] * sizes[1], sizes[2]
    dma = pltpu.SemaphoreType.DMA
    flops = 2 * 27 * width * filters * CELLS
    x_all, act, dy, db = call(
        functools.partial(forward_kernel, sizes, width),
        (
            shape(3, n_chan, part, cells),
            shape(filters, CELLS),
            shape(filters, CELLS),
            shape(8, filters, dtype=F32),
        ),
        4,
        flops,
        10 << 20,
        scratch=(dma((2, 3, n_chan // 2)), dma((2, n_chan)), dma),
        collective_id=0,
    )(own, kernel, bias.reshape(filters, 1), act_grad.reshape(filters, CELLS))
    dw, gx = call(
        functools.partial(grads_kernel, sizes, width),
        (shape(filters, 27 * width), shape(n_chan, planes, part, cells)),
        3,
        3 * flops,
        12 << 20,
        scratch=(pltpu.VMEM((filters, CELLS), BF), dma, dma),
        collective_id=2,
    )(x_all, kernel, dy)
    count = batch * sizes[0]
    rows = filters // group
    slots = pltpu.VMEM((sizes[1], rows, 27 * width), BF)
    dw_all, parts, dbs = call(
        functools.partial(share_kernel, sizes),
        (
            shape(group, rows, 27 * width),
            shape(n_chan, planes, part, cells),
            shape(group, 8, filters, dtype=F32),
        ),
        3,
        0,
        12 << 20,
        scratch=(
            slots,
            slots,
            slots,
            slots,
            dma((3, sizes[1])),
            dma((group,)),
            dma((n_chan,)),
            dma((n_chan,)),
            dma((group,)),
            dma((group,)),
            dma((3,)),
            dma((sizes[1],)),
            dma((sizes[1],)),
            dma((sizes[1],)),
            dma((sizes[1],)),
            dma((sizes[1],)),
        ),
        collective_id=1,
    )(dw.reshape(group, rows, 27 * width), gx, db)
    grad_w = dw_all.reshape(filters, 27 * width).astype(F32) / count
    grad_b = jnp.sum(dbs[:, 0], axis=0) / count
    grad_x = call(merge_kernel, shape(planes * part, cells), 2, 2 * planes * part * cells**2, 1 << 20)(
        parts, parity
    )
    return (
        act.reshape(act_grad.shape),
        grad_x.reshape(volumes.shape),
        grad_w,
        grad_b,
    )


def solution(mesh):
    in_specs = (
        P("dp", "space", "chan", None),
        P("chan", None),
        P("chan"),
        P("dp", "space", "chan", None),
    )
    out_specs = (
        P("dp", "space", "chan", None),
        P("dp", "space", "chan", None),
        P("chan", None),
        P("chan"),
    )
    return jax.shard_map(
        per_device, mesh=mesh, in_specs=in_specs, out_specs=out_specs, check_vma=False
    )
```

```python
import functools

import jax
import jax.numpy as jnp
from jax import lax
from jax.experimental import pallas as pl
from jax.experimental.pallas import tpu as pltpu
from jax.sharding import PartitionSpec as P

GRID = 32
HALF = GRID // 2
CELLS = HALF * HALF
BF = jnp.bfloat16
F32 = jnp.float32
VM = pl.BlockSpec(memory_space=pltpu.VMEM)
TAPS = [(k1, k2, k3) for k1 in range(3) for k2 in range(3) for k3 in range(3)]


def phase_of(k2, k3):
    return 2 * (k2 != 1) + (k3 != 1)


def shift_of(k2, k3):
    return 2 * (k2 == 0) + (k3 == 0)


def parity_matrix():
    full = GRID * GRID
    dst = lax.broadcasted_iota(jnp.int32, (1, full), 1)
    phase, cell = dst // CELLS, dst % CELLS
    y = 2 * (cell // HALF) + phase // 2
    z = 2 * (cell % HALF) + phase % 2
    src = y * GRID + z
    rows = lax.broadcasted_iota(jnp.int32, (full, full), 0)
    return jnp.where(rows == src, 1.0, 0.0).astype(BF)


def lanes():
    return lax.broadcasted_iota(jnp.int32, (1, CELLS), 1)


def forward_shift(x, s):
    if s & 2:
        x = jnp.where(lanes() >= HALF, pltpu.roll(x, HALF, 1), 0.0)
    if s & 1:
        x = jnp.where(lanes() % HALF != 0, pltpu.roll(x, 1, 1), 0.0)
    return x


def backward_shift(x, s):
    if s & 2:
        x = jnp.where(lanes() < CELLS - HALF, pltpu.roll(x, CELLS - HALF, 1), 0.0)
    if s & 1:
        x = jnp.where(lanes() % HALF != HALF - 1, pltpu.roll(x, CELLS - 1, 1), 0.0)
    return x


def split_kernel(v_ref, p_ref, o_ref):
    o_ref[...] = jnp.dot(v_ref[...], p_ref[...], preferred_element_type=F32).astype(BF)


def merge_kernel(v_ref, p_ref, o_ref):
    total = v_ref[0].astype(F32)
    for j in range(1, v_ref.shape[0]):
        total = total + v_ref[j].astype(F32)
    o_ref[...] = lax.dot_general(
        total.astype(BF).reshape(o_ref.shape), p_ref[...], (((1,), (1,)), ((), ())), preferred_element_type=F32
    ).astype(BF)


def send(src, dst, send_sem, recv_sem, device):
    return pltpu.make_async_remote_copy(
        src, dst, send_sem, recv_sem, device_id=device, device_id_type=pl.DeviceIdType.MESH
    )


def place():
    return lax.axis_index("dp"), lax.axis_index("space"), lax.axis_index("chan")


def greet(sizes):
    n_dp, n_space, n_chan = sizes
    y, z, c = place()
    barrier = pltpu.get_barrier_semaphore()
    g = y * n_space + z
    for o in range(1, n_chan):
        pl.semaphore_signal(
            barrier, 1, device_id=(y, z, (c + o) % n_chan), device_id_type=pl.DeviceIdType.MESH
        )
    for o in range(1, n_dp * n_space):
        h = (g + o) % (n_dp * n_space)
        pl.semaphore_signal(
            barrier, 1, device_id=(h // n_space, h % n_space, c), device_id_type=pl.DeviceIdType.MESH
        )
    pl.semaphore_wait(barrier, n_chan + n_dp * n_space - 2)


def gather_inputs(sizes, own_ref, x_ref, out_sem, in_sem, local_sem):
    n_dp, n_space, n_chan = sizes
    chips = n_chan // 2
    y, z, c = place()
    chip, core = c // 2, c % 2
    twin = (y, z, 2 * chip + 1 - core)
    greet(sizes)

    def planes(k):
        return pl.ds(1, 2) if k else pl.ds(0, 1)

    def block(k, j):
        return x_ref.at[planes(k), j]

    def to_chip(k, o, src):
        return send(
            src, block(k, c), out_sem.at[k, 0, o], in_sem.at[k, c],
            (y, z, 2 * ((chip + o) % chips) + core),
        )

    def to_twin(k, o, src):
        j = 2 * ((chip - o + chips) % chips) + core
        return send(src, block(k, j), out_sem.at[k, 1, o], in_sem.at[k, j], twin)

    def arrived(k, j):
        send(block(k, j), block(k, j), out_sem.at[k, 1, 0], in_sem.at[k, j], twin).wait_recv()

    rim = send(own_ref.at[pl.ds(1, 1)], block(0, c), out_sem.at[0, 2, 0], in_sem.at[0, c], (y, jnp.minimum(z + 1, n_space - 1), c))
    sends = [to_chip(1, o, own_ref) for o in range(1, chips)] + [to_twin(1, 0, own_ref)]

    @pl.when(z < n_space - 1)
    def _():
        rim.start()

    for copy in sends:
        copy.start()
    keep = pltpu.make_async_copy(own_ref, block(1, c), local_sem)
    keep.start()

    rim_out = [to_chip(0, o, block(0, c)) for o in range(1, chips)] + [to_twin(0, 0, block(0, c))]

    @pl.when(z > 0)
    def _():
        arrived(0, c)
        for copy in rim_out:
            copy.start()

    @pl.when(z == 0)
    def _():
        x_ref[0] = jnp.zeros_like(x_ref[0])

    for o in range(1, chips):
        j = 2 * ((chip - o + chips) % chips) + core
        arrived(1, j)
        passed = to_twin(1, o, block(1, j))
        passed.start()
        sends.append(passed)

    @pl.when(z > 0)
    def _():
        for o in range(1, chips):
            j = 2 * ((chip - o + chips) % chips) + core
            arrived(0, j)
            passed = to_twin(0, o, block(0, j))
            passed.start()
            rim_out.append(passed)
        for o in range(chips):
            arrived(0, 2 * ((chip - o + chips) % chips) + 1 - core)
        for copy in rim_out:
            copy.wait_send()

    for o in range(chips):
        arrived(1, 2 * ((chip - o + chips) % chips) + 1 - core)
    for copy in sends:
        copy.wait_send()

    @pl.when(z < n_space - 1)
    def _():
        rim.wait_send()

    keep.wait()


def forward_kernel(
    sizes, width, own_ref, w_ref, b_ref, g_ref, x_ref, act_ref, dy_ref, db_ref, out_sem, in_sem, local_sem
):
    gather_inputs(sizes, own_ref, x_ref, out_sem, in_sem, local_sem)
    sums = [None] * 4
    for t, (k1, k2, k3) in enumerate(TAPS):
        ph, s = phase_of(k2, k3), shift_of(k2, k3)
        part = jnp.dot(
            w_ref[:, t * width : (t + 1) * width],
            x_ref[k1, :, :, ph * CELLS : (ph + 1) * CELLS].reshape(width, CELLS),
            preferred_element_type=F32,
        )
        sums[s] = part if sums[s] is None else sums[s] + part
    u = b_ref[...] + sums[0]
    for s in (1, 2, 3):
        u = u + forward_shift(sums[s], s)
    c = 0.7978845608028654
    th = jnp.tanh(c * (u + 0.044715 * (u * u * u)))
    act_ref[...] = (0.5 * u * (1.0 + th)).astype(BF)
    slope = 0.5 * (1.0 + th) + 0.5 * u * (1.0 - th * th) * c * (1.0 + 3 * 0.044715 * u * u)
    dy = (g_ref[...].astype(F32) * slope).astype(BF)
    dy_ref[...] = dy
    db_ref[...] = lax.dot_general(
        jnp.ones((8, CELLS), BF), dy, (((1,), (1,)), ((), ())), preferred_element_type=F32
    )


def shifted(dy):
    wide = dy.astype(F32)
    return [dy] + [backward_shift(wide, s).astype(BF) for s in (1, 2, 3)]


def grads_kernel(sizes, width, x_ref, w_ref, dy_ref, dw_ref, gx_ref, next_ref, out_sem, in_sem):
    n_space = sizes[1]
    y, z, c = place()
    greet(sizes)
    back = send(dy_ref, next_ref, out_sem, in_sem, (y, jnp.maximum(z - 1, 0), c))

    @pl.when(z > 0)
    def _():
        back.start()

    own = shifted(dy_ref[...])
    for t, (k1, k2, k3) in enumerate(TAPS):
        ph, s = phase_of(k2, k3), shift_of(k2, k3)
        part = lax.dot_general(
            own[s],
            x_ref[k1, :, :, ph * CELLS : (ph + 1) * CELLS].reshape(width, CELLS),
            (((1,), (1,)), ((), ())),
            preferred_element_type=F32,
        )
        dw_ref[:, t * width : (t + 1) * width] = part.astype(BF)

    @pl.when(z < n_space - 1)
    def _():
        back.wait_recv()

    @pl.when(z == n_space - 1)
    def _():
        next_ref[...] = jnp.zeros_like(next_ref)

    following = shifted(next_ref[...])
    for plane in range(2):
        for ph in range(4):
            total = None
            for t, (k1, k2, k3) in enumerate(TAPS):
                if phase_of(k2, k3) != ph or (k1 == 1) != (plane == 0):
                    continue
                views = following if k1 == 0 else own
                part = lax.dot_general(
                    w_ref[:, t * width : (t + 1) * width],
                    views[shift_of(k2, k3)],
                    (((0,), (0,)), ((), ())),
                    preferred_element_type=F32,
                )
                total = part if total is None else total + part
            gx_ref[:, plane, :, ph * CELLS : (ph + 1) * CELLS] = total.astype(BF).reshape(
                gx_ref.shape[0], gx_ref.shape[2], CELLS
            )

    @pl.when(z > 0)
    def _():
        back.wait_send()


def share_kernel(
    sizes, dw_ref, gx_ref, db_ref, p_ref, all_ref, merged_ref, dbs_ref, parts_ref, y_ref, r_ref, l_ref, s_ref,
    out_sem, in_sem, gx_out, gx_in, db_out, db_in, local_sem, y_out, y_in, z_out, r_in, l_in
):
    n_dp, n_space, n_chan = sizes
    group = n_dp * n_space
    y, z, c = place()
    g = y * n_space + z
    greet(sizes)
    right = (y, jnp.minimum(z + 1, n_space - 1), c)
    left = (y, jnp.maximum(z - 1, 0), c)
    across = (1 - y, z, c)

    def hop(way, device, j, src=None):
        slot = all_ref.at[y * n_space + j]
        return send(slot if src is None else src, slot, out_sem.at[way, j], in_sem.at[y * n_space + j], device)

    def arrived(h):
        send(all_ref.at[h], all_ref.at[h], out_sem.at[2, 0], in_sem.at[h], across).wait_recv()

    locals_ = [
        pltpu.make_async_copy(gx_ref.at[c], parts_ref.at[c], local_sem.at[1]),
        pltpu.make_async_copy(db_ref, dbs_ref.at[g], local_sem.at[2]),
    ]

    def over(j):
        return send(dw_ref.at[(1 - y) * n_space + j], y_ref.at[j], y_out.at[j], y_in.at[j], across)

    def rightward(j):
        return send(s_ref.at[j], r_ref.at[j], z_out.at[j], r_in.at[j], right)

    def leftward(j):
        return send(s_ref.at[j], l_ref.at[j], z_out.at[j], l_in.at[j], left)

    def both(j):
        over(j).wait_recv()
        return dw_ref[y * n_space + j].astype(F32) + y_ref[j].astype(F32)

    for d in range(n_space - 1, 0, -1):
        @pl.when(z + d < n_space)
        def _():
            over(jnp.minimum(z + d, n_space - 1)).start()

        @pl.when(z - d >= 0)
        def _():
            over(jnp.maximum(z - d, 0)).start()

    over(z).start()
    extra = []
    for o in range(1, n_chan):
        to = (c + o) % n_chan
        extra.append(
            send(gx_ref.at[to], parts_ref.at[c], gx_out.at[o], gx_in.at[o], (y, z, to))
        )
    for o in range(1, group):
        to = (g + o) % group
        extra.append(
            send(db_ref, dbs_ref.at[g], db_out.at[o], db_in.at[o], (to // n_space, to % n_space, c))
        )
    for copy in extra:
        copy.start()
    for copy in locals_:
        copy.start()

    for d in range(n_space - 1, 0, -1):
        @pl.when(z + d < n_space)
        def _():
            j = jnp.minimum(z + d, n_space - 1)
            mine = both(j)

            @pl.when(z == 0)
            def _():
                s_ref[j] = mine.astype(BF)

            @pl.when(z > 0)
            def _():
                rightward(j).wait_recv()
                s_ref[j] = (mine + r_ref[j].astype(F32)).astype(BF)

            rightward(j).start()

        @pl.when(z - d >= 0)
        def _():
            j = jnp.maximum(z - d, 0)
            mine = both(j)

            @pl.when(z == n_space - 1)
            def _():
                s_ref[j] = mine.astype(BF)

            @pl.when(z < n_space - 1)
            def _():
                leftward(j).wait_recv()
                s_ref[j] = (mine + l_ref[j].astype(F32)).astype(BF)

            leftward(j).start()

    @pl.when(z == 0)
    def _():
        r_ref[z] = jnp.zeros_like(r_ref[z])

    @pl.when(z == n_space - 1)
    def _():
        l_ref[z] = jnp.zeros_like(l_ref[z])

    @pl.when(z > 0)
    def _():
        rightward(z).wait_recv()

    @pl.when(z < n_space - 1)
    def _():
        leftward(z).wait_recv()

    all_ref[g] = (both(z) + r_ref[z].astype(F32) + l_ref[z].astype(F32)).astype(BF)

    @pl.when(z < n_space - 1)
    def _():
        hop(0, right, z).start()

    @pl.when(z > 0)
    def _():
        hop(1, left, z).start()

    hop(2, across, z).start()
    for o in range(1, n_chan):
        frm = (c - o + n_chan) % n_chan
        send(parts_ref.at[frm], parts_ref.at[frm], gx_out.at[o], gx_in.at[o], (y, z, frm)).wait_recv()
    locals_[0].wait()
    merge_kernel(parts_ref, p_ref, merged_ref)

    for d in range(1, n_space):
        @pl.when(z - d >= 0)
        def _():
            j = jnp.maximum(z - d, 0)
            arrived(y * n_space + j)

            @pl.when(z < n_space - 1)
            def _():
                hop(0, right, j).start()

            hop(2, across, j).start()

        @pl.when(z + d < n_space)
        def _():
            j = jnp.minimum(z + d, n_space - 1)
            arrived(y * n_space + j)

            @pl.when(z > 0)
            def _():
                hop(1, left, j).start()

            hop(2, across, j).start()

    for o in range(1, group):
        frm = (g - o + group) % group
        send(dbs_ref.at[frm], dbs_ref.at[frm], db_out.at[o], db_in.at[o], (frm // n_space, frm % n_space, c)).wait_recv()
    for j in range(n_space):
        arrived((1 - y) * n_space + j)
        hop(2, across, j).wait_send()

        @pl.when((j <= z) & (z < n_space - 1))
        def _():
            hop(0, right, j).wait_send()

        @pl.when((j >= z) & (z > 0))
        def _():
            hop(1, left, j).wait_send()

        over(j).wait_send()

        @pl.when(j > z)
        def _():
            rightward(j).wait_send()

        @pl.when(j < z)
        def _():
            leftward(j).wait_send()

    for copy in extra:
        copy.wait_send()
    locals_[1].wait()


def call(kernel, out_shape, n_in, flops, moved, scratch=(), collective_id=None):
    many = isinstance(out_shape, (tuple, list))
    return pl.pallas_call(
        kernel,
        out_shape=out_shape,
        in_specs=[VM] * n_in,
        out_specs=[VM] * len(out_shape) if many else VM,
        scratch_shapes=scratch,
        compiler_params=pltpu.CompilerParams(
            vmem_limit_bytes=48 << 20,
            collective_id=collective_id,
            has_side_effects=collective_id is not None,
        ),
        cost_estimate=pl.CostEstimate(flops=flops, bytes_accessed=moved, transcendentals=0),
    )


def shape(*dims, dtype=BF):
    return jax.ShapeDtypeStruct(dims, dtype)


def per_device(volumes, kernel, bias, act_grad):
    batch, planes, part, cells = volumes.shape
    filters = kernel.shape[0]
    width = kernel.shape[1] // 27
    parity = parity_matrix()
    own = call(split_kernel, shape(planes * part, cells), 2, 2 * planes * part * cells**2, 1 << 20)(
        volumes.reshape(planes * part, cells), parity
    ).reshape(planes, part, cells)
    sizes = tuple(lax.axis_size(a) for a in ("dp", "space", "chan"))
    group, n_chan = sizes[0] * sizes[1], sizes[2]
    dma = pltpu.SemaphoreType.DMA
    flops = 2 * 27 * width * filters * CELLS
    x_all, act, dy, db = call(
        functools.partial(forward_kernel, sizes, width),
        (
            shape(3, n_chan, part, cells),
            shape(filters, CELLS),
            shape(filters, CELLS),
            shape(8, filters, dtype=F32),
        ),
        4,
        flops,
        10 << 20,
        scratch=(dma((2, 3, n_chan // 2)), dma((2, n_chan)), dma),
        collective_id=0,
    )(own, kernel, bias.reshape(filters, 1), act_grad.reshape(filters, CELLS))
    dw, gx = call(
        functools.partial(grads_kernel, sizes, width),
        (shape(filters, 27 * width), shape(n_chan, planes, part, cells)),
        3,
        3 * flops,
        12 << 20,
        scratch=(pltpu.VMEM((filters, CELLS), BF), dma, dma),
        collective_id=2,
    )(x_all, kernel, dy)
    count = batch * sizes[0]
    rows = filters // group
    slots = pltpu.VMEM((sizes[1], rows, 27 * width), BF)
    dw_all, grad_x, dbs = call(
        functools.partial(share_kernel, sizes),
        (
            shape(group, rows, 27 * width),
            shape(planes * part, cells),
            shape(group, 8, filters, dtype=F32),
        ),
        4,
        2 * planes * part * cells**2,
        12 << 20,
        scratch=(
            pltpu.VMEM((n_chan, planes, part, cells), BF),
            slots,
            slots,
            slots,
            slots,
            dma((3, sizes[1])),
            dma((group,)),
            dma((n_chan,)),
            dma((n_chan,)),
            dma((group,)),
            dma((group,)),
            dma((3,)),
            dma((sizes[1],)),
            dma((sizes[1],)),
            dma((sizes[1],)),
            dma((sizes[1],)),
            dma((sizes[1],)),
        ),
        collective_id=1,
    )(dw.reshape(group, rows, 27 * width), gx, db, parity)
    grad_w = dw_all.reshape(filters, 27 * width).astype(F32) / count
    grad_b = jnp.sum(dbs[:, 0], axis=0) / count
    return (
        act.reshape(act_grad.shape),
        grad_x.reshape(volumes.shape),
        grad_w,
        grad_b,
    )


def solution(mesh):
    in_specs = (
        P("dp", "space", "chan", None),
        P("chan", None),
        P("chan"),
        P("dp", "space", "chan", None),
    )
    out_specs = (
        P("dp", "space", "chan", None),
        P("dp", "space", "chan", None),
        P("chan", None),
        P("chan"),
    )
    return jax.shard_map(
        per_device, mesh=mesh, in_specs=in_specs, out_specs=out_specs, check_vma=False
    )
```
